32 devices in a mesh: row: 4 (over x, core), col: 8 (over z, y).
Axes of the slice: x: 2, y: 2, z: 4, core: 2. Of those that a mesh axis runs over, the one named last changes fastest.
Arguments:
- iterate: bfloat16 [4096, 8192], P('row', 'col'), may hold values from -0.5 to 0.5, as said below
Outputs:
- update: float32 [4096, 8192], P('row', 'col')
The draws below stay inside these ranges and needn't reach their ends.
Inputs may be any that keep to these rules, and one draw needn't show every extreme that they name: One iterate of the orthogonalization.
All inputs are finite; a program needn't handle non-finite values.
Results may differ from the reference program's by a relative error of at most 0.0041.
Values may be sent and summed in bfloat16 or wider, within the bound.
A program may use at most 64 MiB of HBM per device.

```python
import math
import jax
import jax.numpy as jnp

ROWS = 4096
COLS = 8192


def draw_iterate(key, part):
    first = jax.random.fold_in(key, 0)
    values = jax.random.normal(first, (ROWS, COLS), jnp.float32)
    values = jnp.clip(values, -6.0, 6.0) * (0.7 / jnp.sqrt(jnp.float32(COLS)))
    return values.astype(jnp.bfloat16)


def setup_inputs(seed: int = 0) -> dict:
    seeds = jax.random.split(jax.random.key(seed), 2)
    iterate = draw_iterate(jax.random.fold_in(seeds[1], 71), 0)
    return {"iterate": iterate}


coef_a = 3.4445
coef_b = -4.775
coef_c = 2.0315

def reference(iterate):
    gram = jnp.dot(iterate, iterate.T, preferred_element_type=jnp.float32).astype(jnp.bfloat16)
    square = jnp.dot(gram, gram, preferred_element_type=jnp.float32)
    poly = (coef_b * gram.astype(jnp.float32) + coef_c * square).astype(jnp.bfloat16)
    mixed = jnp.dot(poly, iterate, preferred_element_type=jnp.float32)
    return math.sqrt(COLS) * (coef_a * iterate.astype(jnp.float32) + mixed)
```

```python
import functools
import math

import jax
import jax.numpy as jnp
from jax import lax
from jax.experimental import pallas as pl
from jax.experimental.pallas import tpu as pltpu
from jax.sharding import PartitionSpec as P

MESH = pl.DeviceIdType.MESH
coef_a = 3.4445
coef_b = -4.775
coef_c = 2.0315
SLICES = 2
PIECES = 4


def kernel(
    R, C, scale, x_ref, o_ref, xc, zc, rs, g, y,
    sx, qx, sr, qr, sa, qa, sz, qz,
):
    B, W = x_ref.shape
    T = R // 2
    w = 2 * B // C
    hb = B // 2
    nr = hb // SLICES
    f32, bf16 = jnp.float32, jnp.bfloat16

    r, c = lax.axis_index("row"), lax.axis_index("col")
    odd = lax.rem(c, 2)
    p = (1 - odd) * lax.div(c, 2) + odd * (C - 1 - lax.div(c, 2))

    def col_at(q):
        q = lax.rem(q + C, C)
        hi = lax.div(q, C // 2)
        return (1 - hi) * (2 * q) + hi * (2 * (C - 1 - q) + 1)

    def chunk(q):
        return lax.rem(q + 2 * C, C)

    ring = ((r, col_at(p + 1)), (r, col_at(p - 1)))
    mate = (r + 1 - 2 * lax.rem(r, 2), c)

    def peer(j):
        return (lax.rem(r + 2 * j, R), c)

    def rows_of(row):
        return row * B

    def start_of(t):
        return lax.rem(lax.div(r, 2) + t, T) * (2 * B)

    def hops(u, d):
        return C // 2 if u == d else C - 1 - C // 2

    barrier = pltpu.get_barrier_semaphore()
    friends = [ring[0], ring[1], mate] + [peer(j) for j in range(1, T)]
    for f in friends:
        pl.semaphore_signal(barrier, inc=1, device_id=f, device_id_type=MESH)
    pl.semaphore_wait(barrier, len(friends))

    sent = []

    def send(src, dst, ssem, rsem, to):
        cp = pltpu.make_async_remote_copy(
            src_ref=src, dst_ref=dst, send_sem=ssem, recv_sem=rsem,
            device_id=to, device_id_type=MESH,
        )
        cp.start()
        sent.append(cp)

    def wait_recv(ref, rsem):
        pltpu.make_async_remote_copy(
            src_ref=ref, dst_ref=ref, send_sem=rsem, recv_sem=rsem,
            device_id=mate, device_id_type=MESH,
        ).wait_recv()

    def rows(base, n):
        return pl.ds(pl.multiple_of(base, n), n)

    pr = B // PIECES
    here = rows(r * B, B)
    own = pltpu.make_async_copy(x_ref, xc.at[here, :], sx.at[0, 0])
    own.start()
    send(x_ref, xc.at[here, :], sx.at[0, 1], qx.at[0, 1], mate)
    for i in range(PIECES):
        for j in range(1, T):
            send(
                x_ref.at[pl.ds(i * pr, pr), :],
                xc.at[rows(r * B + i * pr, pr), :],
                sx.at[j, i], qx.at[j, i], peer(j),
            )

    def forward_x(i):
        for j in range(1, T):
            src = lax.rem(r + R - 2 * j, R)
            ref = xc.at[rows(src * B + i * pr, pr), :]
            wait_recv(ref, qx.at[j, i])
            send(ref, ref, sx.at[T + j, i], qx.at[T + j, i], mate)

    def finish_x():
        for i in range(PIECES):
            for j in range(1, T):
                src = lax.rem(mate[0] + R - 2 * j, R)
                wait_recv(xc.at[rows(src * B + i * pr, pr), :], qx.at[T + j, i])

    own.wait()
    wait_recv(xc.at[rows(mate[0] * B, B), :], qx.at[0, 1])

    def part(t, q, u):
        return lax.dot_general(
            x_ref[u * hb : (u + 1) * hb, :],
            xc[rows(start_of(t) + q * w, w), :],
            (((1,), (1,)), ((), ())),
            preferred_element_type=f32,
        )

    for t in range(T):
        for s in range(C // 2 + 1):
            for u in range(2):
                for d in range(2):
                    n = hops(u, d)
                    if s >= n:
                        continue
                    q = chunk(p + (n - s)) if d == 0 else chunk(p - (n - s))
                    v = part(t, q, u)
                    buf = rs.at[t, u, d, s]
                    if s > 0:
                        wait_recv(buf, qr.at[t, u, d, s - 1])
                        v = v + buf[...].astype(f32)
                    buf[...] = v.astype(bf16)
                    send(buf, rs.at[t, u, d, s + 1], sr.at[t, u, d, s], qr.at[t, u, d, s], ring[d])
            if t == 0 and 0 < s <= PIECES:
                forward_x(s - 1)
        if t == 0:
            for i in range(min(C // 2, PIECES), PIECES):
                forward_x(i)
        for u in range(2):
            v = part(t, p, u)
            for d in range(2):
                n = hops(u, d)
                buf = rs.at[t, u, d, n]
                wait_recv(buf, qr.at[t, u, d, n - 1])
                v = v + buf[...].astype(f32)
            g[p, t, u * hb : (u + 1) * hb, :] = v.astype(bf16)
        if t == 0:
            finish_x()

    def add_y(q, u, h, first=False):
        rr = pl.ds(u * hb + h * nr, nr)
        v = None
        for t in range(T):
            m = jnp.dot(
                g[q, t, rr, :], xc[rows(start_of(t) + q * w, w), :], preferred_element_type=f32
            )
            v = m if v is None else v + m
        if first:
            y[rr, :] = v
        else:
            y[rr, :] += v

    def send_g(h, u, d, s):
        q = chunk(p - s) if d == 0 else chunk(p + s)
        ref = g.at[q, :, pl.ds(u * hb + h * nr, nr), :]
        send(ref, ref, sa.at[h, u, d, s], qa.at[h, u, d, s], ring[d])

    def zref(row, u, h):
        return zc.at[rows(row * B + u * hb + h * nr, nr), :]

    def forward_z(h, u):
        for j in range(1, T):
            ref = zref(lax.rem(r + R - 2 * j, R), u, h)
            wait_recv(ref, qz.at[h, u, j])
            send(ref, ref, sz.at[h, u, T + j], qz.at[h, u, T + j], mate)

    def finish_z(h, u):
        for j in range(1, T):
            wait_recv(zref(lax.rem(mate[0] + R - 2 * j, R), u, h), qz.at[h, u, T + j])

    for u in range(2):
        for d in range(2):
            send_g(0, u, d, 0)
    for h in range(SLICES):
        for u in range(2):
            add_y(p, u, h, first=True)
        last = C // 2 - 1
        for s in range(last + 1):
            if s == last and h > 0:
                for u in range(2):
                    forward_z(h - 1, u)
            for u in range(2):
                for d in range(2):
                    n = hops(u, d)
                    if s >= n:
                        continue
                    q = chunk(p - 1 - s) if d == 0 else chunk(p + 1 + s)
                    wait_recv(g.at[q, :, pl.ds(u * hb + h * nr, nr), :], qa.at[h, u, d, s])
                    if s + 1 < n:
                        send_g(h, u, d, s + 1)
                    if s == last - 1 and h + 1 < SLICES:
                        send_g(h + 1, u, d, 0)
                    add_y(q, u, h)
        for u in range(2):
            rr = pl.ds(u * hb + h * nr, nr)
            mine = zref(r, u, h)
            mine[...] = y[rr, :].astype(bf16)
            for j in range(1, T):
                send(mine, mine, sz.at[h, u, j], qz.at[h, u, j], peer(j))
            send(mine, mine, sz.at[h, u, 0], qz.at[h, u, 0], mate)

    tile = min(B, 256)

    def add_out(terms, final=False):
        @pl.loop(0, B // tile)
        def _(i):
            rr = rows(i * tile, tile)
            v = jnp.zeros((tile, W), f32)
            for t, e, u, h in terms:
                k = e * B + u * hb + h * nr
                for k0 in range(k, k + nr, min(w, nr)):
                    n = min(w, nr)
                    q, off = k0 // w, k0 % w
                    v = v + jnp.dot(
                        g[q, t, rr, off : off + n],
                        zc[rows(start_of(t) + k0, n), :],
                        preferred_element_type=f32,
                    )
            if final:
                o_ref[rr, :] = scale * (y[rr, :] + coef_c * v)
            else:
                y[rr, :] += coef_c * v

    @pl.loop(0, B // tile)
    def _(i):
        rr = rows(i * tile, tile)
        y[rr, :] = coef_a * x_ref[rr, :].astype(f32) + coef_b * y[rr, :]

    L = SLICES - 1
    for h in range(SLICES):
        for u in range(2):
            wait_recv(zref(mate[0], u, h), qz.at[h, u, 0])
    for h in range(L):
        for u in range(2):
            finish_z(h, u)
    for h in range(SLICES):
        add_out([(0, e, u, h) for e in range(2) for u in range(2)])
    forward_z(L, 0)
    for h in range(L):
        for t in range(1, T):
            add_out([(t, e, u, h) for e in range(2) for u in range(2)])
    forward_z(L, 1)
    finish_z(L, 0)
    for t in range(1, T):
        add_out([(t, e, 0, L) for e in range(2)])
    finish_z(L, 1)
    for t in range(1, T):
        add_out([(t, e, 1, L) for e in range(2)], final=t == T - 1)

    for cp in sent:
        cp.wait_send()


def solution(mesh):
    R, C = mesh.shape["row"], mesh.shape["col"]

    def step(x):
        B, W = x.shape
        T = R // 2
        w = 2 * B // C
        dma = pltpu.SemaphoreType.DMA
        bf16 = jnp.bfloat16
        rs_sems = (T, 2, 2, C // 2)
        ag_sems = (SLICES, 2, 2, C // 2)
        return pl.pallas_call(
            functools.partial(kernel, R, C, math.sqrt(W * C)),
            out_shape=jax.ShapeDtypeStruct((B, W), jnp.float32),
            in_specs=[pl.BlockSpec(memory_space=pltpu.VMEM)],
            out_specs=pl.BlockSpec(memory_space=pltpu.VMEM),
            scratch_shapes=[
                pltpu.VMEM((R * B, W), bf16),
                pltpu.VMEM((R * B, W), bf16),
                pltpu.VMEM((T, 2, 2, C // 2 + 1, B // 2, w), bf16),
                pltpu.VMEM((C, T, B, w), bf16),
                pltpu.VMEM((B, W), jnp.float32),
                dma((2 * T, PIECES)), dma((2 * T, PIECES)),
                dma(rs_sems), dma(rs_sems),
                dma(ag_sems), dma(ag_sems),
                dma((SLICES, 2, 2 * T)), dma((SLICES, 2, 2 * T)),
            ],
            compiler_params=pltpu.CompilerParams(
                collective_id=0, has_side_effects=True, vmem_limit_bytes=67043328
            ),
        )(x)

    return jax.shard_map(
        step, mesh=mesh, in_specs=(P("row", "col"),), out_specs=P("row", "col"), check_vma=False
    )
```

```python
import functools
import math

import jax
import jax.numpy as jnp
from jax import lax
from jax.experimental import pallas as pl
from jax.experimental.pallas import tpu as pltpu
from jax.sharding import PartitionSpec as P

MESH = pl.DeviceIdType.MESH
coef_a = 3.4445
coef_b = -4.775
coef_c = 2.0315
SLICES = 4
PIECES = 4


def split(B, C):
    w = 2 * B // C
    f = 2 if w % 256 == 0 else 1
    return f, w // f


def kernel(
    R, C, scale, x_ref, o_ref, xc, zc, rs, g, y,
    sx, qx, sr, qr, sa, qa, sz, qz,
):
    B, W = x_ref.shape
    T = R // 2
    HF, ww = split(B, C)
    hb = B // 2
    nr = hb // SLICES
    half = C // 2
    f32, bf16 = jnp.float32, jnp.bfloat16

    r, c = lax.axis_index("row"), lax.axis_index("col")
    odd = lax.rem(c, 2)
    p = (1 - odd) * lax.div(c, 2) + odd * (C - 1 - lax.div(c, 2))

    def col_at(q):
        q = lax.rem(q + C, C)
        hi = lax.div(q, C // 2)
        return (1 - hi) * (2 * q) + hi * (2 * (C - 1 - q) + 1)

    def chunk(q):
        return lax.rem(q + 2 * C, C)

    ring = ((r, col_at(p + 1)), (r, col_at(p - 1)))
    mate = (r + 1 - 2 * lax.rem(r, 2), c)

    def peer(j):
        return (lax.rem(r + 2 * j, R), c)

    def rows_of(row):
        return row * B

    def start_of(t):
        return lax.rem(lax.div(r, 2) + t, T) * (2 * B)

    def hops(u, d):
        return C // 2 if u == d else C - 1 - C // 2

    barrier = pltpu.get_barrier_semaphore()
    friends = [ring[0], ring[1], mate] + [peer(j) for j in range(1, T)]
    for f in friends:
        pl.semaphore_signal(barrier, inc=1, device_id=f, device_id_type=MESH)
    pl.semaphore_wait(barrier, len(friends))

    sent = []

    def send(src, dst, ssem, rsem, to):
        cp = pltpu.make_async_remote_copy(
            src_ref=src, dst_ref=dst, send_sem=ssem, recv_sem=rsem,
            device_id=to, device_id_type=MESH,
        )
        cp.start()
        sent.append(cp)

    def wait_recv(ref, rsem):
        pltpu.make_async_remote_copy(
            src_ref=ref, dst_ref=ref, send_sem=rsem, recv_sem=rsem,
            device_id=mate, device_id_type=MESH,
        ).wait_recv()

    def rows(base, n):
        return pl.ds(pl.multiple_of(base, n), n)

    pr = B // PIECES
    here = rows(r * B, B)
    own = pltpu.make_async_copy(x_ref, xc.at[here, :], sx.at[0, 0])
    own.start()
    send(x_ref, xc.at[here, :], sx.at[0, 1], qx.at[0, 1], mate)
    for i in range(PIECES):
        for j in range(1, T):
            send(
                x_ref.at[pl.ds(i * pr, pr), :],
                xc.at[rows(r * B + i * pr, pr), :],
                sx.at[j, i], qx.at[j, i], peer(j),
            )

    def forward_x(i):
        for j in range(1, T):
            src = lax.rem(r + R - 2 * j, R)
            ref = xc.at[rows(src * B + i * pr, pr), :]
            wait_recv(ref, qx.at[j, i])
            send(ref, ref, sx.at[T + j, i], qx.at[T + j, i], mate)

    def finish_x(i):
        for j in range(1, T):
            src = lax.rem(mate[0] + R - 2 * j, R)
            wait_recv(xc.at[rows(src * B + i * pr, pr), :], qx.at[T + j, i])

    own.wait()
    wait_recv(xc.at[rows(mate[0] * B, B), :], qx.at[0, 1])

    def at(t, f, q):
        e, o = lax.div(q, half), lax.rem(q, half)
        return rows(start_of(t) + e * B + f * (B // HF) + o * ww, ww)

    phases = [(0, f) for f in range(HF)] + [(t, f) for f in range(HF) for t in range(1, T)]
    per = PIECES // HF
    if HF == 2:
        pass_on = {(0, 2): 0, (1, 0): 1, (1, half - 1): 2, (2, 1): 3}
    else:
        pass_on = {(0, i): i for i in range(PIECES)}
    ready = {HF + f * (T - 1): range(f * per, (f + 1) * per) for f in range(HF)}

    side = min(hb, 256)

    def add_part(k, q, u, came, dst):
        t, f = phases[k]

        @pl.loop(0, hb // side)
        def _(i):
            v = lax.dot_general(
                x_ref[rows(u * hb + i * side, side), :],
                xc[at(t, f, q), :],
                (((1,), (1,)), ((), ())),
                preferred_element_type=f32,
            )
            for ref in came:
                v = v + ref[rows(i * side, side), :].astype(f32)
            dst[rows(i * side, side), :] = v.astype(bf16)

    def send_part(k, u, d, s):
        buf = rs.at[k, u, d, s]
        add_part(k, toward(u, d, s), u, [buf] if s else [], buf)
        send(buf, rs.at[k, u, d, s + 1], sr.at[k, u, d, s], qr.at[k, u, d, s], ring[d])

    def toward(u, d, s):
        n = hops(u, d)
        return chunk(p + (n - s)) if d == 0 else chunk(p - (n - s))

    def begin(k):
        for i in ready.get(k, ()):
            finish_x(i)
        for u in range(2):
            for d in range(2):
                send_part(k, u, d, 0)

    begin(0)
    for k, (t, f) in enumerate(phases):
        if (k, 0) in pass_on:
            forward_x(pass_on[k, 0])
        for s in range(1, half):
            for u in range(2):
                for d in range(2):
                    if s < hops(u, d):
                        wait_recv(rs.at[k, u, d, s], qr.at[k, u, d, s - 1])
                        send_part(k, u, d, s)
            if (k, s) in pass_on:
                forward_x(pass_on[k, s])
        if k + 1 < len(phases):
            begin(k + 1)
        for u in range(2):
            came = [rs.at[k, u, d, hops(u, d)] for d in range(2)]
            for d in range(2):
                wait_recv(came[d], qr.at[k, u, d, hops(u, d) - 1])
            add_part(k, p, u, came, g.at[p, t * HF + f, u * hb : (u + 1) * hb, :])

    def dots(left, right):
        if ww % 128 == 0:
            left, right = [jnp.concatenate(left, axis=1)], [jnp.concatenate(right, axis=0)]
        v = None
        for a, b in zip(left, right):
            m = jnp.dot(a, b, preferred_element_type=f32)
            v = m if v is None else v + m
        return v

    def add_y(q, u, h, first=False):
        rr = pl.ds(u * hb + h * nr, nr)
        tf = [(t, f) for t in range(T) for f in range(HF)]
        v = dots([g[q, t * HF + f, rr, :] for t, f in tf], [xc[at(t, f, q), :] for t, f in tf])
        if first:
            y[rr, :] = v
        else:
            y[rr, :] += v

    def send_g(h, u, d, s):
        q = chunk(p - s) if d == 0 else chunk(p + s)
        ref = g.at[q, :, pl.ds(u * hb + h * nr, nr), :]
        send(ref, ref, sa.at[h, u, d, s], qa.at[h, u, d, s], ring[d])

    def zref(row, u, h):
        return zc.at[rows(row * B + u * hb + h * nr, nr), :]

    def forward_z(h, u):
        for j in range(1, T):
            ref = zref(lax.rem(r + R - 2 * j, R), u, h)
            wait_recv(ref, qz.at[h, u, j])
            send(ref, ref, sz.at[h, u, T + j], qz.at[h, u, T + j], mate)

    def finish_z(h, u):
        for j in range(1, T):
            wait_recv(zref(lax.rem(mate[0] + R - 2 * j, R), u, h), qz.at[h, u, T + j])

    tile = min(B, 256)

    def add_out(t, e, h, first=False, final=False):
        terms = {}
        for u in range(2):
            for k0 in range(u * hb + h * nr, u * hb + (h + 1) * nr, ww):
                f, o = k0 // (B // HF), k0 % (B // HF)
                terms.setdefault(e * half + o // ww, []).append((f, e * B + k0))

        @pl.loop(0, B // tile)
        def _(i):
            rr = rows(i * tile, tile)
            v = None
            for q, fs in terms.items():
                m = dots(
                    [g[q, t * HF + f, rr, :] for f, _ in fs],
                    [zc[rows(start_of(t) + k0, ww), :] for _, k0 in fs],
                )
                v = m if v is None else v + m
            if not first:
                v = v + o_ref[rr, :]
            if final:
                v = coef_a * x_ref[rr, :].astype(f32) + coef_b * y[rr, :] + coef_c * v
                v = scale * v
            o_ref[rr, :] = v

    def mate_z(h):
        for u in range(2):
            wait_recv(zref(mate[0], u, h), qz.at[h, u, 0])

    def far_out(h, final=False):
        for u in range(2):
            finish_z(h, u)
        for t in range(1, T):
            for e in range(2):
                add_out(t, e, h, final=final and t == T - 1 and e == 1)

    for u in range(2):
        for d in range(2):
            send_g(0, u, d, 0)
    last = half - 1
    for h in range(SLICES):
        for u in range(2):
            add_y(p, u, h, first=True)
        for s in range(half):
            if s == last and h > 0:
                for u in range(2):
                    forward_z(h - 1, u)
            for u in range(2):
                for d in range(2):
                    n = hops(u, d)
                    if s >= n:
                        continue
                    q = chunk(p - 1 - s) if d == 0 else chunk(p + 1 + s)
                    wait_recv(g.at[q, :, pl.ds(u * hb + h * nr, nr), :], qa.at[h, u, d, s])
                    if s + 1 < n:
                        send_g(h, u, d, s + 1)
                    if s == last - 1 and h + 1 < SLICES:
                        send_g(h + 1, u, d, 0)
                    add_y(q, u, h)
        for u in range(2):
            rr = pl.ds(u * hb + h * nr, nr)
            mine = zref(r, u, h)
            mine[...] = y[rr, :].astype(bf16)
            for j in range(1, T):
                send(mine, mine, sz.at[h, u, j], qz.at[h, u, j], peer(j))
            send(mine, mine, sz.at[h, u, 0], qz.at[h, u, 0], mate)

    L = SLICES - 1
    for h in range(L):
        mate_z(h)
        for e in range(2):
            add_out(0, e, h, first=h == 0 and e == 0)
    far_out(0)
    forward_z(L, 0)
    for h in range(1, L):
        far_out(h)
    forward_z(L, 1)
    mate_z(L)
    for e in range(2):
        add_out(0, e, L)
    far_out(L, final=True)

    for cp in sent:
        cp.wait_send()


def solution(mesh):
    R, C = mesh.shape["row"], mesh.shape["col"]

    def step(x):
        B, W = x.shape
        T = R // 2
        HF, ww = split(B, C)
        dma = pltpu.SemaphoreType.DMA
        bf16 = jnp.bfloat16
        rs_sems = (T * HF, 2, 2, C // 2)
        ag_sems = (SLICES, 2, 2, C // 2)
        return pl.pallas_call(
            functools.partial(kernel, R, C, math.sqrt(W * C)),
            out_shape=jax.ShapeDtypeStruct((B, W), jnp.float32),
            in_specs=[pl.BlockSpec(memory_space=pltpu.VMEM)],
            out_specs=pl.BlockSpec(memory_space=pltpu.VMEM),
            scratch_shapes=[
                pltpu.VMEM((R * B, W), bf16),
                pltpu.VMEM((R * B, W), bf16),
                pltpu.VMEM((T * HF, 2, 2, C // 2 + 1, B // 2, ww), bf16),
                pltpu.VMEM((C, T * HF, B, ww), bf16),
                pltpu.VMEM((B, W), jnp.float32),
                dma((2 * T, PIECES)), dma((2 * T, PIECES)),
                dma(rs_sems), dma(rs_sems),
                dma(ag_sems), dma(ag_sems),
                dma((SLICES, 2, 2 * T)), dma((SLICES, 2, 2 * T)),
            ],
            compiler_params=pltpu.CompilerParams(
                collective_id=0, has_side_effects=True, vmem_limit_bytes=67043328
            ),
        )(x)

    return jax.shard_map(
        step, mesh=mesh, in_specs=(P("row", "col"),), out_specs=P("row", "col"), check_vma=False
    )
```
